1024 devices in a mesh: grp: 32 (over z), bal: 32 (over x, y, core).
Axes of the slice: x: 4, y: 4, z: 32, core: 2. Of those that a mesh axis runs over, the one named last changes fastest.
Arguments:
- own_rows: bfloat16 [8192, 32, 512], P(('grp', 'bal')), may hold values from -24 to 24
- work_cotangent: bfloat16 [4096, 32, 512], P(('grp', 'bal')), may hold values from -24 to 24
- seq_lengths: int32 [8192], P('grp'), may hold values from 0 to 32, as said below
- seq_member: int32 [8192], P('grp'), may hold values from -1 to 31, as said below
- w_uvqk: bfloat16 [512, 2048], replicated, may hold values from -0.25 to 0.25
- w_out: bfloat16 [512, 512], replicated, may hold values from -0.25 to 0.25
Outputs:
- member_out: bfloat16 [4096, 32, 512], P(('grp', 'bal'))
- owner_grad: bfloat16 [8192, 32, 512], P(('grp', 'bal'))
- grad_uvqk: float32 [512, 2048], P('bal')
- grad_out: float32 [512, 512], P('bal')
The draws below stay inside these ranges and needn't reach their ends.
Inputs may be any that keep to these rules, and one draw needn't show every extreme that they name: Slots with seq_member -1 are empty. Every member of a group receives exactly 4 sequences; no owner device sends two sequences to the same member; some owner device holds 8 sequences. `seq_lengths`: 0 exactly on empty slots, 1 or more on the others; each group has a sequence of exactly 32 tokens.
All inputs are finite; a program needn't handle non-finite values.
Results may differ from the reference program's by a relative error of at most 0.028.
Values may be sent and summed in bfloat16 or wider, within the bound.
No kernel may reach another device: no remote copies, remote signals or barrier semaphores. Data moves between devices by JAX's collectives and lax.ppermute only.
A program may use at most 32 MiB of HBM per device.

```python
import math
import jax
import jax.numpy as jnp
from jax import lax

D = 512
HEADS = 8
LEN = 32
WORK = 4
WIDE = 2048
OWN = 8
GROUPS = 32
MEMBERS = 32
NSEQ = 8192
NWORK = 4096
N_GRP = 32
N_BAL = 32


def plan_group(group_key):
    subkeys = jax.random.split(group_key, 7)
    pair_order = jax.random.permutation(subkeys[0], MEMBERS)
    shifts = jax.random.randint(subkeys[1], (MEMBERS // 2,), 0, WORK + 1).astype(jnp.int32)
    shifts = shifts.at[0].set(WORK)
    owner_loads = jnp.zeros((MEMBERS,), jnp.int32)
    owner_loads = owner_loads.at[pair_order[0::2]].set(WORK + shifts)
    owner_loads = owner_loads.at[pair_order[1::2]].set(WORK - shifts)
    owner_order = jax.random.permutation(subkeys[2], MEMBERS)
    ordered_loads = owner_loads[owner_order]
    load_ends = jnp.cumsum(ordered_loads).astype(jnp.int32)
    entries = jnp.arange(MEMBERS * WORK, dtype=jnp.int32)
    placed = jnp.searchsorted(load_ends, entries, side='right').astype(jnp.int32)
    owners = owner_order[placed]
    within = entries - (load_ends - ordered_loads)[placed]
    column_member = jax.random.permutation(subkeys[3], MEMBERS).astype(jnp.int32)
    member = column_member[entries % MEMBERS]
    slots_perm = jax.vmap(lambda one_key: jax.random.permutation(one_key, OWN))(jax.random.split(subkeys[4], MEMBERS))
    slots = slots_perm[owners, within].astype(jnp.int32)
    targets = jnp.full((MEMBERS, OWN), -1, jnp.int32).at[owners, slots].set(member)
    entry_lengths = jax.random.randint(subkeys[5], (MEMBERS * WORK,), 1, LEN + 1).astype(jnp.int32)
    longest = jax.random.randint(subkeys[6], (), 0, MEMBERS * WORK)
    entry_lengths = jnp.where(entries == longest, LEN, entry_lengths).astype(jnp.int32)
    lengths = jnp.zeros((MEMBERS, OWN), jnp.int32).at[owners, slots].set(entry_lengths)
    return (targets.reshape(-1), lengths.reshape(-1))


def plan_all(key):
    base_key = jax.random.fold_in(key, 7177)
    group_keys = jax.random.split(base_key, GROUPS)
    targets, lengths = jax.vmap(plan_group)(group_keys)
    return (targets.reshape(-1), lengths.reshape(-1))


def draw_seq_member(key, part):
    return plan_all(key)[0]


def draw_seq_lengths(key, part):
    return plan_all(key)[1]


def spiked(values, key, source, target, blocks, factor):
    owner, partner = [(jnp.arange(values.shape[dim]) // (values.shape[dim] // blocks)).reshape([-1 if axis == dim else 1 for axis in range(values.ndim)]) for dim in (source, target)]
    chosen = jax.random.permutation(key, blocks)[partner]
    strong = (owner == chosen) | (owner == (partner + blocks // 2) % blocks)
    return jnp.where(strong, factor * values, values)


def steps_of(key, shape, cuts, least, top_value):
    loudness, own = 1.0, jax.random.fold_in(key, 6)
    for dim, blocks in cuts:
        heights = jnp.exp(jax.random.uniform(jax.random.fold_in(own, dim), (blocks,), jnp.float32, least / len(cuts), top_value / len(cuts)))
        loudness = loudness * jnp.repeat(heights, shape[dim] // blocks).reshape([-1 if axis == dim else 1 for axis in range(len(shape))])
    return loudness


def noise(key, dims, scale, bound, cuts=(), kind=jnp.bfloat16):
    values = scale * jax.random.normal(key, dims, jnp.float32)
    if cuts:
        values = values * steps_of(key, dims, cuts, -0.22, 0.18)
    return jnp.clip(values, -bound, bound).astype(kind)


def noise_with(key, dims, scale, limit, cuts, heavy, kind=jnp.bfloat16):
    drawn = scale * jax.random.normal(key, dims, jnp.float32)
    if cuts:
        drawn = drawn * steps_of(key, dims, cuts, -0.22, 0.18)
    return jnp.clip(spiked(drawn, jax.random.fold_in(key, 3), *heavy), -limit, limit).astype(kind)


def setup_inputs(seed: int = 0) -> dict:
    keys = jax.random.split(jax.random.key(seed), 7)
    own_rows = noise_with(keys[0], (NSEQ, LEN, D), 1.0, 24.0, ((0, 1024),), (0, 2, 512, 6.0))
    work_cotangent = noise_with(keys[1], (NWORK, LEN, D), 1.0, 24.0, ((0, 1024),), (0, 2, 512, 6.0))
    seq_lengths = draw_seq_lengths(jax.random.fold_in(keys[6], 71), 0)
    seq_member = draw_seq_member(jax.random.fold_in(keys[6], 71), 0)
    w_uvqk = noise(keys[4], (D, WIDE), D ** -0.5, 0.25)
    w_out = noise(keys[5], (D, D), D ** -0.5, 0.25)
    return dict(own_rows=own_rows, work_cotangent=work_cotangent, seq_lengths=seq_lengths, seq_member=seq_member, w_uvqk=w_uvqk, w_out=w_out)


EPSILON = 1e-05

def norm_rows(values):
    centred = values - lax.optimization_barrier(jnp.mean(values, axis=-1, keepdims=True))
    spread = lax.optimization_barrier(jnp.mean(centred * centred, axis=-1, keepdims=True))
    return centred * lax.rsqrt(spread + EPSILON)

def silu_slope(values):
    sigma = jax.nn.sigmoid(values)
    return sigma * (1.0 + values * (1.0 - sigma))

def mix_rows(activated, lengths):
    seq_count, seq_span, proj_width = activated.shape
    model_width = proj_width // 4
    head_size = model_width // HEADS
    pieces = activated.reshape(seq_count, seq_span, 4, HEADS, head_size).astype(jnp.float32)
    gate_part = pieces[:, :, 0].reshape(seq_count, seq_span, model_width)
    scores = jnp.einsum('sihe,sjhe->shij', pieces[:, :, 2], pieces[:, :, 3]) / math.sqrt(head_size)
    position = jnp.arange(seq_span)
    causal = (position[None, :] <= position[:, None]).astype(jnp.float32)
    weights = jax.nn.silu(scores) * causal / lengths.astype(jnp.float32)[:, None, None, None]
    weights = lax.optimization_barrier(weights.astype(jnp.bfloat16)).astype(jnp.float32)
    attended = jnp.einsum('shij,sjhe->sihe', weights, pieces[:, :, 1])
    return norm_rows(attended.reshape(seq_count, seq_span, model_width)) * gate_part

def layer_rows(rows_x, rows_grad, lengths, w_uvqk, w_out):
    seq_count, seq_span, model_width = rows_x.shape
    total_rows = seq_count * seq_span
    live_mask = (jnp.arange(seq_span)[None, :] < lengths[:, None]).astype(jnp.float32)[:, :, None]
    rows_float = rows_x.astype(jnp.float32)
    normed = norm_rows(rows_float).astype(jnp.bfloat16).reshape(total_rows, model_width)
    projected = jnp.dot(normed, w_uvqk, preferred_element_type=jnp.float32)
    activated = jax.nn.silu(projected).astype(jnp.bfloat16)

    def mixer(values):
        return mix_rows(values.reshape(seq_count, seq_span, -1), lengths)
    mixed, mixer_back = jax.vjp(mixer, activated)
    mixed_flat = mixed.astype(jnp.bfloat16).reshape(total_rows, model_width)
    result = jnp.dot(mixed_flat, w_out, preferred_element_type=jnp.float32).reshape(seq_count, seq_span, model_width)
    result = ((result + rows_float) * live_mask).astype(jnp.bfloat16)
    grad_live = (rows_grad.astype(jnp.float32) * live_mask).astype(jnp.bfloat16)
    grad_flat = grad_live.reshape(total_rows, model_width)
    grad_mixed = jnp.dot(grad_flat, w_out.T, preferred_element_type=jnp.float32)
    grad_act = mixer_back(grad_mixed.reshape(seq_count, seq_span, model_width))[0]
    grad_proj = (grad_act.astype(jnp.float32) * silu_slope(projected)).astype(jnp.bfloat16)
    grad_normed = jnp.dot(grad_proj, w_uvqk.T, preferred_element_type=jnp.float32)
    _, norm_back = jax.vjp(norm_rows, rows_float)
    grad_rows = norm_back(grad_normed.reshape(seq_count, seq_span, model_width))[0] + grad_live.astype(jnp.float32)
    grad_rows = (grad_rows * live_mask).astype(jnp.bfloat16)
    return (result, grad_rows, (normed, grad_proj, mixed_flat, grad_flat))

def work_sources(targets):
    member_ids = jnp.arange(N_BAL)
    to_member = (targets[None, :] == member_ids[:, None]).astype(jnp.int32)
    position = jnp.cumsum(to_member, axis=1) - 1
    work_ids = jnp.arange(WORK)
    chosen = (to_member[:, None, :] > 0) & (position[:, None, :] == work_ids[None, :, None])
    flat_ids = jnp.arange(targets.shape[0])
    picked = lax.optimization_barrier(jnp.sum(chosen.astype(jnp.int32) * flat_ids[None, None, :], axis=2))
    return picked.reshape(N_BAL * WORK).astype(jnp.int32)

def reference(own_rows, work_cotangent, seq_lengths, seq_member, w_uvqk, w_out):
    group_own = own_rows.reshape(N_GRP, N_BAL * OWN, LEN, D)
    group_grad = work_cotangent.reshape(N_GRP, N_BAL * WORK, LEN, D)
    group_lengths = seq_lengths.reshape(N_GRP, N_BAL * OWN)
    group_targets = seq_member.reshape(N_GRP, N_BAL * OWN)

    def one_group(totals, inputs):
        rows_own, rows_grad, lengths, targets = inputs
        sources = work_sources(targets)
        result, grad_rows, factors = layer_rows(rows_own[sources], rows_grad, lengths[sources], w_uvqk, w_out)
        normed, grad_proj, mixed_flat, grad_flat = factors
        term_uvqk = jnp.dot(normed.T, grad_proj, preferred_element_type=jnp.float32)
        term_out = jnp.dot(mixed_flat.T, grad_flat, preferred_element_type=jnp.float32)
        own_grad = jnp.zeros_like(rows_own).at[sources].set(grad_rows)
        return ((totals[0] + term_uvqk, totals[1] + term_out), (result, own_grad))
    start = (jnp.zeros((D, WIDE), jnp.float32), jnp.zeros((D, D), jnp.float32))
    sums, outputs = lax.scan(one_group, start, (group_own, group_grad, group_lengths, group_targets))
    results, own_grads = outputs
    return (results.reshape(N_GRP * N_BAL * WORK, LEN, D), own_grads.reshape(N_GRP * N_BAL * OWN, LEN, D), sums[0], sums[1])
```

```python
import jax
import jax.numpy as jnp
from jax import lax
from jax.sharding import PartitionSpec as P

HEADS = 8


EPSILON = 1e-05


def norm_rows(values):
    centred = values - jnp.mean(values, axis=-1, keepdims=True)
    spread = jnp.mean(centred * centred, axis=-1, keepdims=True)
    return centred * lax.rsqrt(spread + EPSILON)


def silu_slope(values):
    sigma = jax.nn.sigmoid(values)
    return sigma * (1.0 + values * (1.0 - sigma))


def mix_rows(activated, lengths, head_count):
    seq_count, seq_span, proj_width = activated.shape
    model_width = proj_width // 4
    head_size = model_width // head_count
    pieces = activated.reshape(seq_count, seq_span, 4, head_count, head_size)
    gate_part = pieces[:, :, 0].reshape(seq_count, seq_span, model_width).astype(jnp.float32)
    scores = jnp.einsum(
        "sihe,sjhe->shij", pieces[:, :, 2], pieces[:, :, 3], preferred_element_type=jnp.float32
    )
    scores = scores * head_size ** (-0.5)
    position = jnp.arange(seq_span)
    causal = (position[None, :] <= position[:, None]).astype(jnp.float32)
    weights = jax.nn.silu(scores) * causal / lengths.astype(jnp.float32)[:, None, None, None]
    weights = weights.astype(jnp.bfloat16)
    attended = jnp.einsum(
        "shij,sjhe->sihe", weights, pieces[:, :, 1], preferred_element_type=jnp.float32
    )
    return norm_rows(attended.reshape(seq_count, seq_span, model_width)) * gate_part


def layer_rows(rows_x, rows_grad, lengths, w_uvqk, w_out):
    seq_count, seq_span, model_width = rows_x.shape
    total_rows = seq_count * seq_span
    live_mask = (jnp.arange(seq_span)[None, :] < lengths[:, None]).astype(jnp.float32)[:, :, None]
    rows_float = rows_x.astype(jnp.float32)
    normed = norm_rows(rows_float).astype(jnp.bfloat16).reshape(total_rows, model_width)
    projected = jnp.dot(normed, w_uvqk, preferred_element_type=jnp.float32)
    activated = jax.nn.silu(projected).astype(jnp.bfloat16)

    def mixer(values):
        return mix_rows(values.reshape(seq_count, seq_span, -1), lengths, HEADS)

    mixed, mixer_back = jax.vjp(mixer, activated)
    mixed_flat = mixed.astype(jnp.bfloat16).reshape(total_rows, model_width)
    result = jnp.dot(mixed_flat, w_out, preferred_element_type=jnp.float32).reshape(
        seq_count, seq_span, model_width
    )
    result = ((result + rows_float) * live_mask).astype(jnp.bfloat16)
    grad_live = (rows_grad * live_mask).astype(jnp.bfloat16)
    grad_flat = grad_live.reshape(total_rows, model_width)
    grad_mixed = lax.dot_general(
        grad_flat, w_out, (((1,), (1,)), ((), ())), preferred_element_type=jnp.float32
    )
    grad_act = mixer_back(grad_mixed.reshape(seq_count, seq_span, model_width))[0]
    grad_proj = (grad_act.astype(jnp.float32) * silu_slope(projected)).astype(jnp.bfloat16)
    grad_normed = lax.dot_general(
        grad_proj, w_uvqk, (((1,), (1,)), ((), ())), preferred_element_type=jnp.float32
    )
    _, norm_back = jax.vjp(norm_rows, rows_float)
    grad_rows = norm_back(grad_normed.reshape(seq_count, seq_span, model_width))[
        0
    ] + grad_live.astype(jnp.float32)
    grad_rows = (grad_rows * live_mask).astype(jnp.bfloat16)
    return (result, grad_rows, (normed, grad_proj, mixed_flat, grad_flat))


def swap_pieces(pieces, axis, groups=None):
    return lax.all_to_all(
        pieces, axis, split_axis=0, concat_axis=0, tiled=True, axis_index_groups=groups
    )


def reduce_terms(terms, model_width):
    members = lax.axis_size("bal")
    groups = lax.axis_size("grp")
    chips = members // 2
    rows, width = terms.shape
    part_rows = rows // members
    core_pairs = [[2 * chip, 2 * chip + 1] for chip in range(chips)]
    same_core = [[2 * chip + core for chip in range(chips)] for core in range(2)]
    by_core = terms.reshape(chips, 2, part_rows, width).transpose(1, 0, 2, 3)
    halves = swap_pieces(by_core.reshape(2, chips * part_rows, width), "bal", core_pairs)
    chip_sum = jnp.sum(halves.astype(jnp.float32), axis=0).astype(jnp.bfloat16)
    slices = swap_pieces(chip_sum.reshape(chips, part_rows, width), "bal", same_core)
    part = jnp.sum(slices.astype(jnp.float32), axis=0).astype(jnp.bfloat16)
    pair_rows, cuts = 2, groups * 2 // part_rows
    pieces = part.reshape(part_rows // pair_rows, pair_rows, cuts, width // cuts)
    pieces = pieces.transpose(0, 2, 1, 3).reshape(groups, pair_rows, width // cuts)
    piece = jnp.sum(swap_pieces(pieces, "grp").astype(jnp.float32), axis=0).astype(jnp.bfloat16)
    spread = swap_pieces(jnp.broadcast_to(piece[None], pieces.shape), "grp")
    total = spread.reshape(part_rows // pair_rows, cuts, pair_rows, width // cuts)
    total = total.transpose(0, 2, 1, 3).reshape(part_rows, width).astype(jnp.float32)
    return total[:, : width - model_width], total[:, width - model_width :]


def body(own_rows, work_cotangent, seq_lengths, seq_member, w_uvqk, w_out):
    members = lax.axis_size("bal")
    my_index = lax.axis_index("bal")
    own_count, seq_span, model_width = own_rows.shape
    work_count = work_cotangent.shape[0]
    pair_cap = -(-own_count // members)
    item_count = members * pair_cap
    member_of = seq_member.reshape(members, own_count)
    length_of = seq_lengths.reshape(members, own_count)
    slot_ids = jnp.arange(own_count)
    same_member = (member_of[:, :, None] == member_of[:, None, :]) & (
        slot_ids[None, None, :] < slot_ids[None, :, None]
    )
    pair_rank = jnp.sum(same_member.astype(jnp.int32), axis=2)
    my_members = lax.dynamic_index_in_dim(member_of, my_index, 0, keepdims=False)
    my_ranks = lax.dynamic_index_in_dim(pair_rank, my_index, 0, keepdims=False)
    item_ids = jnp.arange(item_count)
    send_pick = ((my_members * pair_cap + my_ranks)[None, :] == item_ids[:, None]) & (
        my_members >= 0
    )[None, :]
    send_pick = send_pick.astype(jnp.bfloat16)
    outgoing = jnp.dot(
        send_pick,
        own_rows.reshape(own_count, seq_span * model_width),
        preferred_element_type=jnp.float32,
    )
    incoming = lax.all_to_all(
        outgoing.astype(jnp.bfloat16), "bal", split_axis=0, concat_axis=0, tiled=True
    )
    to_me = member_of == my_index
    rank_ids = jnp.arange(pair_cap)
    hit_table = (to_me[:, :, None] & (pair_rank[:, :, None] == rank_ids[None, None, :])).astype(
        jnp.int32
    )
    item_live = jnp.sum(hit_table, axis=1).reshape(item_count)
    item_length = jnp.sum(hit_table * length_of[:, :, None], axis=1).reshape(item_count)
    position = jnp.cumsum(item_live) - 1
    work_ids = jnp.arange(work_count)
    pick_work = (item_live[None, :] > 0) & (position[None, :] == work_ids[:, None])
    work_rows = jnp.dot(
        pick_work.astype(jnp.bfloat16), incoming, preferred_element_type=jnp.float32
    )
    work_rows = work_rows.astype(jnp.bfloat16).reshape(work_count, seq_span, model_width)
    work_lengths = jnp.sum(pick_work.astype(jnp.int32) * item_length[None, :], axis=1)
    result, grad_rows, factors = layer_rows(work_rows, work_cotangent, work_lengths, w_uvqk, w_out)
    normed, grad_proj, mixed_flat, grad_flat = factors
    back_items = lax.dot_general(
        pick_work.astype(jnp.bfloat16),
        grad_rows.reshape(work_count, seq_span * model_width),
        (((0,), (0,)), ((), ())),
        preferred_element_type=jnp.float32,
    )
    returned = lax.all_to_all(
        back_items.astype(jnp.bfloat16), "bal", split_axis=0, concat_axis=0, tiled=True
    )
    own_grad = lax.dot_general(
        send_pick, returned, (((0,), (0,)), ((), ())), preferred_element_type=jnp.float32
    )
    own_grad = own_grad.astype(jnp.bfloat16).reshape(own_count, seq_span, model_width)
    term_uvqk = lax.dot_general(
        normed, grad_proj, (((0,), (0,)), ((), ())), preferred_element_type=jnp.float32
    )
    term_out = lax.dot_general(
        mixed_flat, grad_flat, (((0,), (0,)), ((), ())), preferred_element_type=jnp.float32
    )
    terms = jnp.concatenate([term_uvqk, term_out], axis=1).astype(jnp.bfloat16)
    grad_uvqk, grad_out = reduce_terms(terms, model_width)
    return (result, own_grad, grad_uvqk, grad_out)


def solution(mesh):
    placed = (
        P(("grp", "bal"), None, None),
        P(("grp", "bal"), None, None),
        P("grp"),
        P("grp"),
        P(),
        P(),
    )
    return jax.shard_map(
        body,
        mesh=mesh,
        in_specs=placed,
        out_specs=(
            P(("grp", "bal"), None, None),
            P(("grp", "bal"), None, None),
            P("bal", None),
            P("bal", None),
        ),
        check_vma=False,
    )
```

```python
import jax
import jax.numpy as jnp
from jax import lax
from jax.experimental import pallas as pl
from jax.experimental.pallas import tpu as pltpu
from jax.sharding import PartitionSpec as P

HEADS = 8


EPSILON = 1e-05


def row_stats(values):
    centred = values - jnp.mean(values, axis=-1, keepdims=True)
    scale = lax.rsqrt(jnp.mean(centred * centred, axis=-1, keepdims=True) + EPSILON)
    return centred * scale, scale


def norm_back(hat, scale, grad):
    drop = jnp.mean(grad, axis=-1, keepdims=True)
    slant = jnp.mean(grad * hat, axis=-1, keepdims=True)
    return scale * (grad - drop - hat * slant)


def dot(left, right, contract):
    return lax.dot_general(
        left, right, ((contract[:1], contract[1:]), ((), ())), preferred_element_type=jnp.float32
    )


def send_kernel(member_ref, index_ref, rows_ref, out_ref):
    own_count = rows_ref.shape[0]
    start = index_ref[0] * own_count
    for slot in range(own_count):
        member = member_ref[start + slot]

        @pl.when(member >= 0)
        def _():
            out_ref[jnp.maximum(member, 0)] = rows_ref[slot]


def send_rows(seq_member, index, own_rows, members):
    own_count, seq_span, model_width = own_rows.shape
    return pl.pallas_call(
        send_kernel,
        grid_spec=pltpu.PrefetchScalarGridSpec(
            num_scalar_prefetch=2,
            grid=(1,),
            in_specs=[pl.BlockSpec(own_rows.shape, lambda i, m, x: (0, 0, 0))],
            out_specs=pl.BlockSpec(
                (members, seq_span, model_width), lambda i, m, x: (0, 0, 0)
            ),
        ),
        out_shape=jax.ShapeDtypeStruct((members, seq_span, model_width), own_rows.dtype),
    )(seq_member, index, own_rows)


def take_kernel(member_ref, index_ref, back_ref, out_ref, sems):
    own_count = out_ref.shape[0]
    start = index_ref[0] * own_count

    def each(slot, act):
        member = member_ref[start + slot]

        @pl.when(member >= 0)
        def _():
            copy = pltpu.make_async_copy(
                back_ref.at[jnp.maximum(member, 0)], out_ref.at[slot], sems.at[slot]
            )
            act(copy)

        return member

    for slot in range(own_count):
        member = each(slot, lambda copy: copy.start())

        @pl.when(member < 0)
        def _():
            out_ref[slot] = jnp.zeros(out_ref.shape[1:], out_ref.dtype)

    for slot in range(own_count):
        each(slot, lambda copy: copy.wait())


def take_rows(seq_member, index, returned, own_count):
    _, seq_span, model_width = returned.shape
    return pl.pallas_call(
        take_kernel,
        grid_spec=pltpu.PrefetchScalarGridSpec(
            num_scalar_prefetch=2,
            grid=(1,),
            in_specs=[pl.BlockSpec(memory_space=pl.ANY)],
            out_specs=pl.BlockSpec((own_count, seq_span, model_width), lambda i, m, x: (0, 0, 0)),
            scratch_shapes=[pltpu.SemaphoreType.DMA((own_count,))],
        ),
        out_shape=jax.ShapeDtypeStruct((own_count, seq_span, model_width), returned.dtype),
    )(seq_member, index, returned)


def layer_kernel(
    source_ref, length_ref, core_ref,
    incoming_ref, cot_ref, wide_ref, narrow_ref,
    result_ref, back_ref, keep_ref, send_ref,
    x_ref, grad_ref, slope_ref, act_ref, score_ref, att_ref, proj_ref, term_ref, x_sems, out_sems,
):
    work, span, width = cot_ref.shape
    total = work * span
    head_size = width // HEADS
    pair = 2 * head_size
    pairs = HEADS // 2
    f32, bf16 = jnp.float32, jnp.bfloat16
    for p in range(work):
        pltpu.make_async_copy(incoming_ref.at[source_ref[p]], x_ref.at[p], x_sems.at[p]).start()

    row = lax.broadcasted_iota(jnp.int32, (total, 1), 0)
    seq, place = row // span, row % span
    length = jnp.full((total, 1), length_ref[0], jnp.int32)
    for p in range(1, work):
        length = jnp.where(seq == p, length_ref[p], length)
    live = place < length
    inverse = 1.0 / length.astype(f32)
    wide_row = lax.broadcasted_iota(jnp.int32, (total, total), 0)
    wide_col = lax.broadcasted_iota(jnp.int32, (total, total), 1)
    visible = (wide_row // span == wide_col // span) & (wide_col <= wide_row)
    causal = jnp.where(visible, inverse, 0.0)
    low_half = lax.broadcasted_iota(jnp.int32, (total, pair), 1) < head_size

    grad_live = jnp.where(live, cot_ref[...].reshape(total, width).astype(f32), 0.0).astype(bf16)
    grad_mixed = dot(grad_live, narrow_ref[...], (1, 1))

    for p in range(work):
        pltpu.make_async_copy(incoming_ref.at[source_ref[p]], x_ref.at[p], x_sems.at[p]).wait()
    rows = x_ref[...].reshape(total, width).astype(f32)
    hat, scale = row_stats(rows)
    normed = hat.astype(bf16)

    for part in range(4):
        cols = slice(part * width, (part + 1) * width)
        projected = dot(normed, wide_ref[:, cols], (1, 0))
        sigma = jax.nn.sigmoid(projected)
        act_ref[:, cols] = (projected * sigma).astype(bf16)
        slope_ref[:, cols] = sigma * (1.0 + projected * (1.0 - sigma))

    def half(values, which):
        return jnp.where(low_half if which == 0 else ~low_half, values, jnp.zeros_like(values))

    def block(part, g):
        return act_ref[:, part * width + g * pair : part * width + (g + 1) * pair]

    for g in range(pairs):
        value, query, key = block(1, g), block(2, g), block(3, g)
        attended = None
        for which in range(2):
            head = 2 * g + which
            scores = dot(half(query, which), key, (1, 1)) * head_size**-0.5
            score_ref[head] = scores
            weights = (scores * jax.nn.sigmoid(scores) * causal).astype(bf16)
            mixed_in = dot(weights, half(value, which), (1, 0))
            attended = mixed_in if attended is None else attended + mixed_in
        att_ref[:, g * pair : (g + 1) * pair] = attended

    att_hat, att_scale = row_stats(att_ref[...])
    gate = act_ref[:, :width].astype(f32)
    mixed = (att_hat * gate).astype(bf16)
    result = jnp.where(live, dot(mixed, narrow_ref[...], (1, 0)) + rows, 0.0)
    result_ref[...] = result.astype(bf16).reshape(work, span, width)

    def put_terms(values, col, size):
        term_ref[:, :, :, col : col + size] = values.astype(bf16).reshape(
            term_ref.shape[:3] + (size,)
        )

    put_terms(dot(mixed, grad_live, (0, 0)), 4 * width, width)

    grad_act = (grad_mixed * att_hat).astype(bf16).astype(f32)
    proj_ref[:, :width] = (grad_act * slope_ref[:, :width]).astype(bf16)
    grad_att = norm_back(att_hat, att_scale, grad_mixed * gate).astype(bf16)

    for g in range(pairs):
        value, query, key = block(1, g), block(2, g), block(3, g)
        grad_out = grad_att[:, g * pair : (g + 1) * pair]
        sums = [None, None, None]
        for which in range(2):
            head = 2 * g + which
            scores = score_ref[head]
            sigma = jax.nn.sigmoid(scores)
            weights = (scores * sigma * causal).astype(bf16)
            grad_half = half(grad_out, which)
            grad_weights = dot(grad_half, value, (1, 1))
            grad_scores = (
                grad_weights * causal * (sigma * (1.0 + scores * (1.0 - sigma))) * head_size**-0.5
            ).astype(bf16)
            grads = (
                dot(weights, grad_half, (0, 0)),
                dot(grad_scores, half(key, which), (1, 0)),
                dot(grad_scores, half(query, which), (0, 0)),
            )
            sums = [b if a is None else a + b for a, b in zip(sums, grads)]
        for part, grad in enumerate(sums):
            cols = slice((part + 1) * width + g * pair, (part + 1) * width + (g + 1) * pair)
            grad = grad.astype(bf16).astype(f32)
            proj_ref[:, cols] = (grad * slope_ref[:, cols]).astype(bf16)

    for part in range(4):
        cols = slice(part * width, (part + 1) * width)
        put_terms(dot(normed, proj_ref[:, cols], (0, 0)), part * width, width)
    core = core_ref[0]
    copies = [
        pltpu.make_async_copy(term_ref.at[:, core], keep_ref, out_sems.at[0]),
        pltpu.make_async_copy(term_ref.at[:, 1 - core], send_ref, out_sems.at[1]),
    ]
    for copy in copies:
        copy.start()

    grad_normed = dot(proj_ref[...], wide_ref[...], (1, 1))
    grad_rows = norm_back(hat, scale, grad_normed) + grad_live.astype(f32)
    grad_rows = jnp.where(live, grad_rows, 0.0).astype(bf16)
    grad_ref[...] = grad_rows.reshape(work, span, width)
    for p in range(work):
        copies.append(
            pltpu.make_async_copy(grad_ref.at[p], back_ref.at[source_ref[p]], out_sems.at[2 + p])
        )
        copies[-1].start()
    for copy in copies:
        copy.wait()


def run_layer(source, lengths, core, incoming, cotangent, w_uvqk, w_out):
    work, span, width = cotangent.shape
    members = incoming.shape[0]
    total, wide = work * span, w_uvqk.shape[1]
    part_rows, chips = width // members, members // 2
    whole = pl.BlockSpec(memory_space=pltpu.VMEM)
    far = pl.BlockSpec(memory_space=pl.ANY)
    bf16, f32 = jnp.bfloat16, jnp.float32
    half_terms = jax.ShapeDtypeStruct((chips, part_rows, wide + width), bf16)
    return pl.pallas_call(
        layer_kernel,
        grid_spec=pltpu.PrefetchScalarGridSpec(
            num_scalar_prefetch=3,
            grid=(1,),
            in_specs=[far, whole, whole, whole],
            out_specs=[whole, far, far, far],
            scratch_shapes=[
                pltpu.VMEM((work, span, width), bf16),
                pltpu.VMEM((work, span, width), bf16),
                pltpu.VMEM((total, wide), f32),
                pltpu.VMEM((total, wide), bf16),
                pltpu.VMEM((HEADS, total, total), f32),
                pltpu.VMEM((total, width), f32),
                pltpu.VMEM((total, wide), bf16),
                pltpu.VMEM((chips, 2, part_rows, wide + width), bf16),
                pltpu.SemaphoreType.DMA((work,)),
                pltpu.SemaphoreType.DMA((2 + work,)),
            ],
        ),
        out_shape=[
            jax.ShapeDtypeStruct(cotangent.shape, bf16),
            jax.ShapeDtypeStruct(incoming.shape, bf16),
            half_terms,
            half_terms,
        ],
    )(source, lengths, core, incoming, cotangent, w_uvqk, w_out)


def swap_pieces(pieces, axis, groups=None):
    return lax.all_to_all(
        pieces, axis, split_axis=0, concat_axis=0, tiled=True, axis_index_groups=groups
    )


def sum_pieces(pieces):
    return jnp.sum(pieces.astype(jnp.float32), axis=0).astype(jnp.bfloat16)


def reduce_terms(keep, send, model_width):
    members = lax.axis_size("bal")
    groups = lax.axis_size("grp")
    chips, part_rows, width = keep.shape
    same_core = [[2 * chip + core for chip in range(chips)] for core in range(2)]
    received = lax.ppermute(send, "bal", [(m, m ^ 1) for m in range(members)])
    chip_sum = (keep.astype(jnp.float32) + received.astype(jnp.float32)).astype(jnp.bfloat16)
    part = sum_pieces(swap_pieces(chip_sum, "bal", same_core))
    near, far = 4, groups // 4
    near_groups = [[near * block + i for i in range(near)] for block in range(far)]
    far_groups = [[near * block + i for block in range(far)] for i in range(near)]
    pieces = part.reshape(part_rows, near, width // near).transpose(1, 0, 2)
    piece = sum_pieces(swap_pieces(pieces, "grp", near_groups))
    copies = jnp.broadcast_to(piece[None], (far,) + piece.shape)
    piece = sum_pieces(swap_pieces(copies, "grp", far_groups))
    copies = jnp.broadcast_to(piece[None], (near,) + piece.shape)
    total = swap_pieces(copies, "grp", near_groups)
    total = total.transpose(1, 0, 2).reshape(part_rows, width).astype(jnp.float32)
    return total[:, : width - model_width], total[:, width - model_width :]


def work_sources(seq_lengths, seq_member, my_index, own_count, work_count):
    members = seq_member.shape[0] // own_count
    to_me = (seq_member.reshape(members, own_count) == my_index).astype(jnp.int32)
    owns = jnp.sum(to_me, axis=1)
    item_length = jnp.sum(to_me * seq_lengths.reshape(members, own_count), axis=1)
    ids = jnp.arange(members)
    position = jnp.sum(jnp.where(ids[None, :] < ids[:, None], owns[None, :], 0), axis=1)
    picked = (owns[None, :] > 0) & (position[None, :] == jnp.arange(work_count)[:, None])
    picked = picked.astype(jnp.int32)
    source = jnp.sum(picked * ids[None, :].astype(jnp.int32), axis=1)
    return source, jnp.sum(picked * item_length[None, :], axis=1)


def body(own_rows, work_cotangent, seq_lengths, seq_member, w_uvqk, w_out):
    members = lax.axis_size("bal")
    my_index = lax.axis_index("bal").astype(jnp.int32)
    own_count, _, model_width = own_rows.shape
    work_count = work_cotangent.shape[0]
    index = my_index[None]
    incoming = swap_pieces(send_rows(seq_member, index, own_rows, members), "bal")
    source, lengths = work_sources(seq_lengths, seq_member, my_index, own_count, work_count)
    result, back, keep, send = run_layer(
        source, lengths, index % 2, incoming, work_cotangent, w_uvqk, w_out
    )
    own_grad = take_rows(seq_member, index, swap_pieces(back, "bal"), own_count)
    grad_uvqk, grad_out = reduce_terms(keep, send, model_width)
    return (result, own_grad, grad_uvqk, grad_out)


def solution(mesh):
    placed = (
        P(("grp", "bal"), None, None),
        P(("grp", "bal"), None, None),
        P("grp"),
        P("grp"),
        P(),
        P(),
    )
    return jax.shard_map(
        body,
        mesh=mesh,
        in_specs=placed,
        out_specs=(
            P(("grp", "bal"), None, None),
            P(("grp", "bal"), None, None),
            P("bal", None),
            P("bal", None),
        ),
        check_vma=False,
    )
```

```python
import jax
import jax.numpy as jnp
from jax import lax
from jax.experimental import pallas as pl
from jax.experimental.pallas import tpu as pltpu
from jax.sharding import PartitionSpec as P

HEADS = 8


EPSILON = 1e-05


def row_stats(values):
    centred = values - jnp.mean(values, axis=-1, keepdims=True)
    scale = lax.rsqrt(jnp.mean(centred * centred, axis=-1, keepdims=True) + EPSILON)
    return centred * scale, scale


def norm_back(hat, scale, grad):
    drop = jnp.mean(grad, axis=-1, keepdims=True)
    slant = jnp.mean(grad * hat, axis=-1, keepdims=True)
    return scale * (grad - drop - hat * slant)


def dot(left, right, contract):
    return lax.dot_general(
        left, right, ((contract[:1], contract[1:]), ((), ())), preferred_element_type=jnp.float32
    )


def send_kernel(member_ref, index_ref, cot_ref, out_ref):
    members = out_ref.shape[0]
    own_count = member_ref.shape[0] // members
    work_count = cot_ref.shape[0]
    mine = index_ref[0]

    def each(owner, place):
        found = member_ref[owner * own_count] == mine
        for slot in range(1, own_count):
            found = found | (member_ref[owner * own_count + slot] == mine)

        @pl.when(found)
        def _():
            out_ref[owner] = cot_ref[jnp.minimum(place, work_count - 1)]

        return place + found.astype(jnp.int32)

    lax.fori_loop(0, members, each, jnp.int32(0))


def send_cotangent(seq_member, index, cotangent, members):
    _, seq_span, model_width = cotangent.shape
    return pl.pallas_call(
        send_kernel,
        grid_spec=pltpu.PrefetchScalarGridSpec(
            num_scalar_prefetch=2,
            grid=(1,),
            in_specs=[pl.BlockSpec(cotangent.shape, lambda i, m, x: (0, 0, 0))],
            out_specs=pl.BlockSpec(
                (members, seq_span, model_width), lambda i, m, x: (0, 0, 0)
            ),
        ),
        out_shape=jax.ShapeDtypeStruct((members, seq_span, model_width), cotangent.dtype),
    )(seq_member, index, cotangent)


def take_kernel(source_ref, back_ref, out_ref):
    for place in range(out_ref.shape[0]):
        out_ref[place] = back_ref[source_ref[place]]


def take_result(source, returned, work_count):
    _, seq_span, model_width = returned.shape
    whole = pl.BlockSpec(memory_space=pltpu.VMEM)
    return pl.pallas_call(
        take_kernel,
        grid_spec=pltpu.PrefetchScalarGridSpec(
            num_scalar_prefetch=1, grid=(1,), in_specs=[whole], out_specs=whole
        ),
        out_shape=jax.ShapeDtypeStruct((work_count, seq_span, model_width), returned.dtype),
    )(source, returned)


def row_lengths(length_ref, start, own_count, span):
    seq = lax.broadcasted_iota(jnp.int32, (own_count * span, 1), 0) // span
    place = lax.broadcasted_iota(jnp.int32, (own_count * span, 1), 0) % span
    length = jnp.full((own_count * span, 1), length_ref[start], jnp.int32)
    for slot in range(1, own_count):
        length = jnp.where(seq == slot, length_ref[start + slot], length)
    return length, place < length


def forward_kernel(
    member_ref, length_ref, index_ref,
    rows_ref, wide_ref, narrow_ref,
    slots_ref, act_ref, slope_ref, weight_ref, bend_ref, att_ref, mixed_ref,
    result_ref, sems,
):
    own_count, span, width = rows_ref.shape
    total = own_count * span
    square = weight_ref.shape[-1]
    head_size = width // HEADS
    pair = 2 * head_size
    f32, bf16 = jnp.float32, jnp.bfloat16
    start = index_ref[0] * own_count
    length, live = row_lengths(length_ref, start, own_count, span)
    inverse = jnp.where(length > 0, 1.0 / jnp.maximum(length, 1).astype(f32), 0.0)
    wide_row = lax.broadcasted_iota(jnp.int32, (square, square), 0)
    wide_col = lax.broadcasted_iota(jnp.int32, (square, square), 1)
    visible = (wide_row // span == wide_col // span) & (wide_col <= wide_row)
    low_half = lax.broadcasted_iota(jnp.int32, (square, pair), 1) < head_size

    rows = rows_ref[...].reshape(total, width).astype(f32)
    normed = row_stats(rows)[0].astype(bf16)
    for part in range(4):
        cols = slice(part * width, (part + 1) * width)
        projected = dot(normed, wide_ref[:, cols], (1, 0))
        sigma = jax.nn.sigmoid(projected)
        act_ref[:, cols] = (projected * sigma).astype(bf16)
        slope_ref[:, cols] = (sigma * (1.0 + projected * (1.0 - sigma))).astype(bf16)

    for cut in range(total // square):
        span_rows = slice(cut * square, (cut + 1) * square)
        causal = jnp.where(visible, inverse[span_rows], 0.0)
        for g in range(HEADS // 2):
            value, query, key = (
                act_ref[span_rows, part * width + g * pair : part * width + (g + 1) * pair]
                for part in (1, 2, 3)
            )
            attended = None
            for which in range(2):
                keep = low_half if which == 0 else ~low_half
                scores = dot(jnp.where(keep, query, 0), key, (1, 1)) * head_size**-0.5
                sigma = jax.nn.sigmoid(scores)
                weights = (scores * sigma * causal).astype(bf16)
                weight_ref[cut, 2 * g + which] = weights
                bend = sigma * (1.0 + scores * (1.0 - sigma)) * causal * head_size**-0.5
                bend_ref[cut, 2 * g + which] = bend.astype(bf16)
                part_sum = dot(weights, jnp.where(keep, value, 0), (1, 0))
                attended = part_sum if attended is None else attended + part_sum
            att_ref[span_rows, g * pair : (g + 1) * pair] = attended

    att_hat, _ = row_stats(att_ref[...])
    mixed = (att_hat * act_ref[:, :width].astype(f32)).astype(bf16)
    mixed_ref[...] = mixed
    result = jnp.where(live, dot(mixed, narrow_ref[...], (1, 0)) + rows, 0.0)
    result_ref[...] = result.astype(bf16).reshape(own_count, span, width)

    for act in ("start", "wait"):
        for slot in range(own_count):
            member = member_ref[start + slot]

            @pl.when(member >= 0)
            def _():
                copy = pltpu.make_async_copy(
                    result_ref.at[slot], slots_ref.at[jnp.maximum(member, 0)], sems.at[slot]
                )
                getattr(copy, act)()


def run_forward(seq_member, seq_lengths, index, own_rows, w_uvqk, w_out, members):
    own_count, span, width = own_rows.shape
    total, wide = own_count * span, w_uvqk.shape[1]
    square = min(128, total)
    whole = pl.BlockSpec(memory_space=pltpu.VMEM)
    far = pl.BlockSpec(memory_space=pl.ANY)
    bf16, f32 = jnp.bfloat16, jnp.float32
    squares = jax.ShapeDtypeStruct((total // square, HEADS, square, square), bf16)
    return pl.pallas_call(
        forward_kernel,
        grid_spec=pltpu.PrefetchScalarGridSpec(
            num_scalar_prefetch=3,
            grid=(1,),
            in_specs=[whole, whole, whole],
            out_specs=[far] + [whole] * 6,
            scratch_shapes=[
                pltpu.VMEM((own_count, span, width), bf16),
                pltpu.SemaphoreType.DMA((own_count,)),
            ],
        ),
        out_shape=[
            jax.ShapeDtypeStruct((members, span, width), bf16),
            jax.ShapeDtypeStruct((total, wide), bf16),
            jax.ShapeDtypeStruct((total, wide), bf16),
            squares,
            squares,
            jax.ShapeDtypeStruct((total, width), f32),
            jax.ShapeDtypeStruct((total, width), bf16),
        ],
    )(seq_member, seq_lengths, index, own_rows, w_uvqk, w_out)


def backward_kernel(
    member_ref, length_ref, index_ref,
    incoming_ref, rows_ref, wide_ref, narrow_ref,
    act_ref, slope_ref, weight_ref, bend_ref, att_ref, mixed_ref,
    grad_ref, keep_ref, send_ref,
    cot_ref, proj_ref, term_ref, out_sems,
):
    own_count, span, width = rows_ref.shape
    total = own_count * span
    square = weight_ref.shape[-1]
    head_size = width // HEADS
    pair = 2 * head_size
    f32, bf16 = jnp.float32, jnp.bfloat16
    start = index_ref[0] * own_count
    _, live = row_lengths(length_ref, start, own_count, span)
    low_half = lax.broadcasted_iota(jnp.int32, (square, pair), 1) < head_size

    for slot in range(own_count):
        cot_ref[slot] = incoming_ref[jnp.maximum(member_ref[start + slot], 0)]
    cot = cot_ref[...].reshape(total, width).astype(f32)
    grad_live = jnp.where(live, cot, 0.0).astype(bf16)
    grad_mixed = dot(grad_live, narrow_ref[...], (1, 1))

    def put_terms(values, col, size):
        term_ref[:, :, :, col : col + size] = values.astype(bf16).reshape(
            term_ref.shape[:3] + (size,)
        )

    put_terms(dot(mixed_ref[...], grad_live, (0, 0)), 4 * width, width)

    att_hat, att_scale = row_stats(att_ref[...])
    gate = act_ref[:, :width].astype(f32)
    grad_act = (grad_mixed * att_hat).astype(bf16).astype(f32)
    proj_ref[:, :width] = (grad_act * slope_ref[:, :width].astype(f32)).astype(bf16)
    grad_att = norm_back(att_hat, att_scale, grad_mixed * gate).astype(bf16)

    for cut in range(total // square):
        span_rows = slice(cut * square, (cut + 1) * square)
        for g in range(HEADS // 2):
            value, query, key = (
                act_ref[span_rows, part * width + g * pair : part * width + (g + 1) * pair]
                for part in (1, 2, 3)
            )
            grad_out = grad_att[span_rows, g * pair : (g + 1) * pair]
            sums = [None, None, None]
            for which in range(2):
                keep = low_half if which == 0 else ~low_half
                grad_half = jnp.where(keep, grad_out, 0)
                grad_weights = dot(grad_half, value, (1, 1))
                bend = bend_ref[cut, 2 * g + which].astype(f32)
                grad_scores = (grad_weights * bend).astype(bf16)
                grads = (
                    dot(weight_ref[cut, 2 * g + which], grad_half, (0, 0)),
                    dot(grad_scores, jnp.where(keep, key, 0), (1, 0)),
                    dot(grad_scores, jnp.where(keep, query, 0), (0, 0)),
                )
                sums = [b if a is None else a + b for a, b in zip(sums, grads)]
            for part, grad in enumerate(sums):
                cols = slice((part + 1) * width + g * pair, (part + 1) * width + (g + 1) * pair)
                grad = grad.astype(bf16).astype(f32)
                proj_ref[span_rows, cols] = (
                    grad * slope_ref[span_rows, cols].astype(f32)
                ).astype(bf16)

    rows = rows_ref[...].reshape(total, width).astype(f32)
    hat, scale = row_stats(rows)
    normed = hat.astype(bf16)
    for part in range(4):
        cols = slice(part * width, (part + 1) * width)
        put_terms(dot(normed, proj_ref[:, cols], (0, 0)), part * width, width)
    core = lax.rem(index_ref[0], 2)
    copies = [
        pltpu.make_async_copy(term_ref.at[:, core], keep_ref, out_sems.at[0]),
        pltpu.make_async_copy(term_ref.at[:, 1 - core], send_ref, out_sems.at[1]),
    ]
    for copy in copies:
        copy.start()

    grad_normed = dot(proj_ref[...], wide_ref[...], (1, 1))
    grad_rows = norm_back(hat, scale, grad_normed) + grad_live.astype(f32)
    grad_rows = jnp.where(live, grad_rows, 0.0).astype(bf16)
    grad_ref[...] = grad_rows.reshape(own_count, span, width)
    for copy in copies:
        copy.wait()


def run_backward(seq_member, seq_lengths, index, incoming, own_rows, w_uvqk, w_out, saved):
    own_count, span, width = own_rows.shape
    members = incoming.shape[0]
    total, wide = own_count * span, w_uvqk.shape[1]
    part_rows, chips = width // members, members // 2
    whole = pl.BlockSpec(memory_space=pltpu.VMEM)
    far = pl.BlockSpec(memory_space=pl.ANY)
    bf16 = jnp.bfloat16
    half_terms = jax.ShapeDtypeStruct((chips, part_rows, wide + width), bf16)
    return pl.pallas_call(
        backward_kernel,
        grid_spec=pltpu.PrefetchScalarGridSpec(
            num_scalar_prefetch=3,
            grid=(1,),
            in_specs=[whole] * (4 + len(saved)),
            out_specs=[whole, far, far],
            scratch_shapes=[
                pltpu.VMEM((own_count, span, width), bf16),
                pltpu.VMEM((total, wide), bf16),
                pltpu.VMEM((chips, 2, part_rows, wide + width), bf16),
                pltpu.SemaphoreType.DMA((2,)),
            ],
        ),
        out_shape=[
            jax.ShapeDtypeStruct(own_rows.shape, bf16),
            half_terms,
            half_terms,
        ],
    )(seq_member, seq_lengths, index, incoming, own_rows, w_uvqk, w_out, *saved)


def swap_pieces(pieces, axis, groups=None):
    return lax.all_to_all(
        pieces, axis, split_axis=0, concat_axis=0, tiled=True, axis_index_groups=groups
    )


def sum_pieces(pieces):
    return jnp.sum(pieces.astype(jnp.float32), axis=0).astype(jnp.bfloat16)


def sum_pair(keep, send):
    members = lax.axis_size("bal")
    received = lax.ppermute(send, "bal", [(m, m ^ 1) for m in range(members)])
    return (keep.astype(jnp.float32) + received.astype(jnp.float32)).astype(jnp.bfloat16)


def reduce_terms(chip_sum, model_width):
    groups = lax.axis_size("grp")
    chips, part_rows, width = chip_sum.shape
    near, far = 4, groups // 4
    same_core = [[2 * chip + core for chip in range(chips)] for core in range(2)]
    near_groups = [[near * block + i for i in range(near)] for block in range(far)]
    far_groups = [[near * block + i for block in range(far)] for i in range(near)]
    part = sum_pieces(swap_pieces(chip_sum, "bal", same_core))
    pieces = part.reshape(part_rows, near, width // near).transpose(1, 0, 2)
    piece = sum_pieces(swap_pieces(pieces, "grp", near_groups))
    copies = jnp.broadcast_to(piece[None], (far,) + piece.shape)
    piece = sum_pieces(swap_pieces(copies, "grp", far_groups))
    copies = jnp.broadcast_to(piece[None], (near,) + piece.shape)
    total = swap_pieces(copies, "grp", near_groups)
    total = total.transpose(1, 0, 2).reshape(part_rows, width).astype(jnp.float32)
    return total[:, : width - model_width], total[:, width - model_width :]


def work_sources(seq_member, my_index, own_count, work_count):
    members = seq_member.shape[0] // own_count
    to_me = (seq_member.reshape(members, own_count) == my_index).astype(jnp.int32)
    owns = jnp.sum(to_me, axis=1)
    ids = jnp.arange(members)
    position = jnp.sum(jnp.where(ids[None, :] < ids[:, None], owns[None, :], 0), axis=1)
    picked = (owns[None, :] > 0) & (position[None, :] == jnp.arange(work_count)[:, None])
    return jnp.sum(picked.astype(jnp.int32) * ids[None, :].astype(jnp.int32), axis=1)


def body(own_rows, work_cotangent, seq_lengths, seq_member, w_uvqk, w_out):
    members = lax.axis_size("bal")
    my_index = lax.axis_index("bal").astype(jnp.int32)
    own_count, _, model_width = own_rows.shape
    work_count = work_cotangent.shape[0]
    index = my_index[None]
    outgoing = send_cotangent(seq_member, index, work_cotangent, members)
    incoming = swap_pieces(outgoing, "bal")
    slots, *saved = run_forward(seq_member, seq_lengths, index, own_rows, w_uvqk, w_out, members)
    returned = swap_pieces(slots, "bal")
    own_grad, keep, send = run_backward(
        seq_member, seq_lengths, index, incoming, own_rows, w_uvqk, w_out, saved
    )
    chip_sum = sum_pair(keep, send)
    returned, chip_sum = lax.optimization_barrier((returned, chip_sum))
    grad_uvqk, grad_out = reduce_terms(chip_sum, model_width)
    source = work_sources(seq_member, my_index, own_count, work_count)
    return (take_result(source, returned, work_count), own_grad, grad_uvqk, grad_out)


def solution(mesh):
    placed = (
        P(("grp", "bal"), None, None),
        P(("grp", "bal"), None, None),
        P("grp"),
        P("grp"),
        P(),
        P(),
    )
    return jax.shard_map(
        body,
        mesh=mesh,
        in_specs=placed,
        out_specs=(
            P(("grp", "bal"), None, None),
            P(("grp", "bal"), None, None),
            P("bal", None),
            P("bal", None),
        ),
        check_vma=False,
    )
```
